32 devices in a mesh: ctx: 8 (over z, x), head: 4 (over y, core).
Axes of the slice: x: 2, y: 2, z: 4, core: 2. Of those that a mesh axis runs over, the one named last changes fastest.
Arguments:
- hidden: bfloat16 [256, 8192], P(None, 'ctx')
- norm_gain: float32 [8192], replicated, may hold values from 0.1 to 1.9
- w_query: bfloat16 [8192, 8192], P('ctx', 'head'), may hold values from -0.0625 to 0.0625
- manifest_keys: bfloat16 [8, 4096, 128], P(None, 'ctx')
- manifest_values: bfloat16 [8, 4096, 128], P(None, 'ctx'), may hold values from -6 to 6
- w_output: bfloat16 [8192, 8192], P('head', 'ctx'), may hold values from -0.0625 to 0.0625
- valid_len: int32 [256], replicated, may hold values from 1 to 4096, as said below
- home_block: int32 [256], replicated, may hold values from 0 to 7, as said below
Outputs:
- projected: float32 [256, 8192], P('head', 'ctx')
The draws below stay inside these ranges and needn't reach their ends.
Inputs may be any that keep to these rules, and one draw needn't show every extreme that they name: `valid_len`: every draw has a row that reads the whole manifest and a row with length 1. `home_block`: every draw assigns some row to the first block and some row to the last.
All inputs are finite; a program needn't handle non-finite values.
Results may differ from the reference program's by a relative error of at most 0.005.
The reference program's roundings to bfloat16 on the way count: a program that leaves them out, or rounds other values in their place, can miss the bound.
Values may be sent and summed in bfloat16 or wider, within the bound.
A program may use at most 128 MiB of HBM per device.

```python
import math
import jax
import jax.numpy as jnp
from jax import lax

D = 8192
H = 64
KVH = 8
HD = 128
L_DEV = 512
ROWS = 256
CTXLEN = 4096
NBLK = 8
GROUP = 8


def draw_hidden(key, part):
    key_base, key_rows, key_cols = jax.random.split(key, 3)
    base = jax.random.normal(key_base, (ROWS, D), jnp.float32)
    row_scale = jnp.exp(jax.random.uniform(key_rows, (ROWS, 1), jnp.float32, 0.0, math.log(10.0)))
    ramp = jnp.exp(math.log(3.0) * jnp.arange(D, dtype=jnp.float32) / D)
    col_scale = jnp.exp(jax.random.uniform(key_cols, (1, D), jnp.float32, 0.0, math.log(5.0))) * ramp[None, :]
    return (base * row_scale * col_scale).astype(jnp.bfloat16)


def draw_manifest_keys(key, part):
    key_base = jax.random.fold_in(key, 0)
    result = jax.random.normal(key_base, (KVH, CTXLEN, HD), jnp.float32) * 3.0
    return result.astype(jnp.bfloat16)


def draw_valid_len(key, part):
    key_len, key_pick = jax.random.split(key, 2)
    lengths = jax.random.randint(key_len, (ROWS,), 1, CTXLEN + 1)
    picked = jax.random.randint(key_pick, (), 0, ROWS)
    lengths = lengths.at[picked].set(CTXLEN)
    lengths = lengths.at[(picked + 1) % ROWS].set(1)
    return lengths.astype(jnp.int32)


def draw_home_block(key, part):
    key_block, key_pick = jax.random.split(key, 2)
    blocks = jax.random.randint(key_block, (ROWS,), 0, NBLK)
    picked = jax.random.randint(key_pick, (), 0, ROWS)
    blocks = blocks.at[picked].set(0)
    blocks = blocks.at[(picked + 1) % ROWS].set(NBLK - 1)
    return blocks.astype(jnp.int32)


def levels(rng, extent, cuts, low, largest):
    def one(position, blocks):
        draws = jax.random.uniform(jax.random.fold_in(jax.random.fold_in(rng, 6), position), (blocks,), jnp.float32, low / len(cuts), largest / len(cuts))
        return jnp.repeat(jnp.exp(draws), extent[position] // blocks).reshape((-1,) + (1,) * (len(extent) - position - 1))

    factor_of = one(*cuts[0])
    for cut in cuts[1:]:
        factor_of = factor_of * one(*cut)
    return factor_of


def gaussian(stream_key, shape, deviation, limit, shards=(), kind=jnp.bfloat16):
    values = deviation * jax.random.normal(stream_key, shape, jnp.float32)
    if shards:
        values = values * levels(stream_key, shape, shards, -0.22, 0.18)
    return jnp.clip(values, -limit, limit).astype(kind)


def setup_inputs(seed: int = 0) -> dict:
    key_of = jax.random.split(jax.random.key(seed), 9)
    return {
        "hidden": draw_hidden(jax.random.fold_in(key_of[8], 71), 0),
        "norm_gain": jnp.clip(1.0 + 0.18 * jax.random.normal(key_of[1], (D,), jnp.float32), 0.1, 1.9),
        "w_query": gaussian(key_of[2], (D, H * HD), D ** -0.5, 0.0625, ((0, 8), (1, 4))),
        "manifest_keys": draw_manifest_keys(jax.random.fold_in(key_of[8], 71), 0),
        "manifest_values": gaussian(key_of[4], (KVH, CTXLEN, HD), 1.0, 6.0, ((1, 8),)),
        "w_output": gaussian(key_of[5], (H * HD, D), (H * HD) ** -0.5, 0.0625, ((0, 4), (1, 8))),
        "valid_len": draw_valid_len(jax.random.fold_in(key_of[8], 71), 0),
        "home_block": draw_home_block(jax.random.fold_in(key_of[8], 71), 0),
    }


def reference(hidden, norm_gain, w_query, manifest_keys, manifest_values, w_output, valid_len, home_block):
    widened = hidden.astype(jnp.float32)
    inv_rms = lax.rsqrt(lax.optimization_barrier(jnp.mean(widened * widened, axis=1, keepdims=True)) + 1e-05)
    normed = (widened * inv_rms * norm_gain[None, :]).astype(jnp.bfloat16)
    query = jnp.dot(normed, w_query, preferred_element_type=jnp.float32).astype(jnp.bfloat16)
    places = jnp.arange(CTXLEN, dtype=jnp.int32)
    usable = (places[None, :] < valid_len[:, None]) | ((places // L_DEV)[None, :] == home_block[:, None])
    by_head = query.reshape(ROWS, H, HD).transpose(1, 0, 2)

    def one_head(head_index):
        q_head = lax.dynamic_index_in_dim(by_head, head_index, 0, keepdims=False)
        kv_index = (head_index // GROUP).astype(jnp.int32)
        key_head = lax.dynamic_index_in_dim(manifest_keys, kv_index, 0, keepdims=False)
        value_head = lax.dynamic_index_in_dim(manifest_values, kv_index, 0, keepdims=False)
        scores = jnp.dot(q_head, key_head.T, preferred_element_type=jnp.float32) * (1.0 / math.sqrt(HD))
        scores = jnp.where(usable, scores, -1e+30)
        row_max = lax.optimization_barrier(jnp.max(scores, axis=1, keepdims=True))
        expo_vals = jnp.where(usable, jnp.exp(scores - row_max), 0.0)
        row_sum = lax.optimization_barrier(jnp.sum(expo_vals, axis=1, keepdims=True))
        weighted = jnp.dot(expo_vals.astype(jnp.bfloat16), value_head, preferred_element_type=jnp.float32)
        return (weighted / row_sum).astype(jnp.bfloat16)
    attn = lax.map(one_head, jnp.arange(H, dtype=jnp.int32))
    attn = attn.transpose(1, 0, 2).reshape(ROWS, H * HD)
    return jnp.dot(attn, w_output, preferred_element_type=jnp.float32)
```

```python
import math

import jax
import jax.numpy as jnp
from jax import lax
from jax.sharding import PartitionSpec as P

H = 64
KVH = 8
HD = 128


def shards(
    hidden, norm_gain, w_query, manifest_keys, manifest_values, w_output, valid_len, home_block
):
    ctx_count = lax.axis_size("ctx")
    ctx_index = lax.axis_index("ctx")
    head_index = lax.axis_index("head")
    rows, feat = hidden.shape
    d_model = feat * ctx_count
    width = w_query.shape[1]
    heads_here = width // HD
    group = H // KVH
    span = manifest_keys.shape[1]
    hsplit = min(ctx_count, heads_here)
    rsplit = ctx_count // hsplit
    rows_dev = rows // rsplit
    heads_dev = heads_here // hsplit

    widened = hidden.astype(jnp.float32)
    total_sq = lax.psum(jnp.sum(widened * widened, axis=1, keepdims=True), "ctx")
    inv_rms = lax.rsqrt(total_sq / d_model + 1e-05)
    gain = lax.dynamic_slice_in_dim(norm_gain, ctx_index * feat, feat, 0)
    normed = (widened * inv_rms * gain[None, :]).astype(jnp.bfloat16)
    partial = jnp.dot(normed, w_query, preferred_element_type=jnp.float32)
    partial = partial.reshape(rsplit, rows_dev, hsplit, heads_dev * HD).transpose(2, 0, 1, 3)
    partial = partial.reshape(ctx_count, rows_dev, heads_dev * HD)
    query = lax.psum_scatter(partial, "ctx", scatter_dimension=0, tiled=False).astype(jnp.bfloat16)

    dest_heads = head_index * heads_here + (jnp.arange(ctx_count) // rsplit) * heads_dev
    dest_kv = dest_heads // group
    kv = jnp.stack([manifest_keys[dest_kv], manifest_values[dest_kv]], axis=1)
    kv = lax.all_to_all(kv, "ctx", split_axis=0, concat_axis=0, tiled=True)
    kv = kv.transpose(1, 0, 2, 3).reshape(2, ctx_count * span, HD)
    keys, values = kv[0], kv[1]

    first_row = (ctx_index % rsplit) * rows_dev
    lens = lax.dynamic_slice_in_dim(valid_len, first_row, rows_dev, 0)
    blocks = lax.dynamic_slice_in_dim(home_block, first_row, rows_dev, 0)
    places = jnp.arange(ctx_count * span, dtype=jnp.int32)
    usable = (places[None, :] < lens[:, None]) | ((places // span)[None, :] == blocks[:, None])
    usable = usable[:, None, :]
    q3 = query.reshape(rows_dev, heads_dev, HD)
    scores = jnp.einsum("nhd,jd->nhj", q3, keys, preferred_element_type=jnp.float32) * (
        1.0 / math.sqrt(HD)
    )
    scores = jnp.where(usable, scores, -1e30)
    row_max = jnp.max(scores, axis=2, keepdims=True)
    expo = jnp.where(usable, jnp.exp(scores - row_max), 0.0)
    row_sum = jnp.sum(expo, axis=2, keepdims=True)
    weighted = jnp.einsum(
        "nhj,jd->nhd", expo.astype(jnp.bfloat16), values, preferred_element_type=jnp.float32
    )
    attn = (weighted / row_sum).astype(jnp.bfloat16).reshape(rows_dev, heads_dev * HD)
    attn = lax.all_gather(attn, "ctx", axis=0, tiled=False)
    attn = attn.reshape(hsplit, rsplit, rows_dev, heads_dev * HD).transpose(1, 2, 0, 3)
    attn = attn.reshape(rows, width)
    return lax.psum_scatter(
        jnp.dot(attn, w_output, preferred_element_type=jnp.float32),
        "head",
        scatter_dimension=0,
        tiled=True,
    )


def solution(mesh):
    in_specs = (
        P(None, "ctx"),
        P(),
        P("ctx", "head"),
        P(None, "ctx", None),
        P(None, "ctx", None),
        P("head", "ctx"),
        P(),
        P(),
    )
    out_specs = P("head", "ctx")
    return jax.shard_map(shards, mesh=mesh, in_specs=in_specs, out_specs=out_specs, check_vma=False)
```

```python
import math

import jax
import jax.numpy as jnp
from jax import lax
from jax.experimental import pallas as pl
from jax.experimental.pallas import tpu as pltpu
from jax.sharding import PartitionSpec as P

H = 64
KVH = 8
HD = 128

Z = 4
X = 2


def fused_kernel(
    hidden, gain, wq_hbm, k_hbm, v_hbm, wo_hbm, lens, home, out,
    wq, wo, kb, vb, vt, nrm, sq, xsend, xrecv, qown, zsend, zrecv, qb, sc,
    os_, st, ocr, scr, az, ax, acc, orecv, local_sem, send_sem, recv_sem,
):
    c = lax.axis_index("ctx")
    h = lax.axis_index("head")
    z, x = lax.div(c, X), lax.rem(c, X)
    nz = lax.axis_size("ctx")
    nh = lax.axis_size("head")
    rows, feat = hidden.shape
    span = kb.shape[1]
    chunk = qb.shape[2]
    half = chunk * Z
    out_rows = out.shape[0]
    per_chunk = chunk // HD
    scale = 1.0 / math.sqrt(HD)
    f32 = jnp.float32
    pending = []
    next_sem = [0]

    def at(zz, xx):
        return zz * X + xx

    def send(src, dst, **where):
        i = next_sem[0]
        next_sem[0] += 1
        copy = pltpu.make_async_remote_copy(
            src_ref=src, dst_ref=dst, send_sem=send_sem.at[i], recv_sem=recv_sem.at[i],
            device_id=where, device_id_type=pl.DeviceIdType.MESH,
        )
        copy.start()
        pending.append(copy)
        return copy

    def zat(k):
        return lax.rem(z + k, Z)

    barrier = pltpu.get_barrier_semaphore()
    for k in range(1, nz):
        pl.semaphore_signal(barrier, inc=1, device_id={"ctx": lax.rem(c + k, nz)}, device_id_type=pl.DeviceIdType.MESH)
    for k in range(1, nh):
        pl.semaphore_signal(barrier, inc=1, device_id={"head": lax.rem(h + k, nh)}, device_id_type=pl.DeviceIdType.MESH)

    kv_mine = h * X + x
    kv_other = h * X + (1 - x)
    locals_ = [
        pltpu.make_async_copy(wq_hbm, wq, local_sem.at[0]),
        pltpu.make_async_copy(k_hbm.at[kv_mine], kb.at[0], local_sem.at[1]),
        pltpu.make_async_copy(v_hbm.at[kv_mine], vb.at[0], local_sem.at[2]),
        pltpu.make_async_copy(wo_hbm, wo, local_sem.at[3]),
    ]
    for cp in locals_:
        cp.start()

    eye = lax.broadcasted_iota(jnp.int32, (128, 128), 0) == lax.broadcasted_iota(jnp.int32, (128, 128), 1)
    wide = hidden[...].astype(f32)
    col = jnp.sum(wide * wide, axis=1, keepdims=True)
    pieces = [
        jnp.sum(jnp.where(eye, col[b * 128 : (b + 1) * 128], 0.0), axis=0, keepdims=True)
        for b in range(rows // 128)
    ]
    pieces.append(jnp.zeros((8 - rows // 128, 128), f32))
    sq[0] = jnp.concatenate(pieces, axis=0)
    pl.semaphore_wait(barrier, nz - 1 + nh - 1)
    sq_copies = [send(sq.at[0], sq.at[k], ctx=lax.rem(c + k, nz)) for k in range(1, nz)]
    zp = z + 1 - 2 * lax.rem(z, 2)
    kv_copies = []
    for slot, (idx, zz, xx) in enumerate(((kv_other, z, 1 - x), (kv_mine, zp, x), (kv_other, zp, 1 - x)), 1):
        kv_copies.append(send(k_hbm.at[idx], kb.at[slot], ctx=at(zz, xx)))
        kv_copies.append(send(v_hbm.at[idx], vb.at[slot], ctx=at(zz, xx)))
    for cp in sq_copies:
        cp.wait_recv()
    total = sq[0]
    for k in range(1, nz):
        total = total + sq[k]
    inv = lax.rsqrt(total / (feat * nz) + 1e-05)
    for b in range(rows // 128):
        inv_col = jnp.sum(jnp.where(eye, inv[b : b + 1, :], 0.0), axis=1, keepdims=True)
        blk = hidden[b * 128 : (b + 1) * 128, :].astype(f32)
        g = gain[:, pl.ds(pl.multiple_of(c * feat, feat), feat)]
        nrm[b * 128 : (b + 1) * 128, :] = (blk * inv_col * g).astype(jnp.bfloat16)

    def part(xx, k):
        cols = pl.ds(pl.multiple_of(xx * half + zat(k) * chunk, chunk), chunk)
        return jnp.dot(nrm[...], wq[:, cols], preferred_element_type=f32)

    locals_[0].wait()
    x_copies = {}
    for k in (1, 2, 3, 0):
        xsend[k] = part(1 - x, k)
        x_copies[k] = send(xsend.at[k], xrecv.at[k], ctx=at(z, 1 - x))
    for k in (1, 2, 3, 0):
        qown[k] = part(x, k)
    z_copies = []
    for k in (1, 2, 3):
        x_copies[k].wait_recv()
        zsend[k - 1] = qown[k] + xrecv[k]
        z_copies.append(send(zsend.at[k - 1], zrecv.at[k - 1], ctx=at(zat(k), x)))

    locals_[1].wait()
    locals_[2].wait()
    for cp in kv_copies:
        cp.wait_recv()
    for s in range(4):
        vt[s] = vb[s].astype(f32).T.astype(jnp.bfloat16)

    x_copies[0].wait_recv()
    qsum = qown[0] + xrecv[0]
    for k in range(3):
        z_copies[k].wait_recv()
        qsum = qsum + zrecv[k]
    qb[0] = qsum.astype(jnp.bfloat16)
    far = at(zat(2), x)
    q_copy = send(qb.at[0], qb.at[1], ctx=far)

    place = lax.broadcasted_iota(jnp.int32, (span, rows), 0)
    owners = (at(z, x), at(z, 1 - x), at(zp, x), at(zp, 1 - x))

    def attend(i):
        for j in range(per_chunk):
            q_head = qb[i, :, j * HD : (j + 1) * HD]
            top = jnp.full((1, rows), -1e30, f32)
            for s in range(4):
                limit = jnp.where(home[...] == owners[s], span, lens[...] - owners[s] * span)
                raw = lax.dot_general(kb[s], q_head, (((1,), (1,)), ((), ())), preferred_element_type=f32)
                raw = jnp.where(place < limit, raw, -1e30)
                sc[s] = raw
                top = jnp.maximum(top, jnp.max(raw, axis=0, keepdims=True))
            tot = jnp.zeros((1, rows), f32)
            acc_o = jnp.zeros((HD, rows), f32)
            for s in range(4):
                e = jnp.exp((sc[s] - top) * scale)
                tot = tot + jnp.sum(e, axis=0, keepdims=True)
                acc_o = acc_o + jnp.dot(vt[s], e.astype(jnp.bfloat16), preferred_element_type=f32)
            os_[i, j] = acc_o
            st[i, j : j + 1, :] = top
            st[i, per_chunk + j : per_chunk + j + 1, :] = tot

    st[...] = jnp.zeros_like(st)
    attend(0)
    q_copy.wait_recv()
    attend(1)
    o_copy = send(os_.at[1], ocr, ctx=far)
    s_copy = send(st.at[1], scr, ctx=far)
    o_copy.wait_recv()
    s_copy.wait_recv()
    for j in range(per_chunk):
        m0, m1 = st[0, j : j + 1, :], scr[j : j + 1, :]
        l0, l1 = st[0, per_chunk + j : per_chunk + j + 1, :], scr[per_chunk + j : per_chunk + j + 1, :]
        m = jnp.maximum(m0, m1)
        a0, a1 = jnp.exp((m0 - m) * scale), jnp.exp((m1 - m) * scale)
        res = (a0 * os_[0, j] + a1 * ocr[j]) / (a0 * l0 + a1 * l1)
        az[0, :, j * HD : (j + 1) * HD] = res.T.astype(jnp.bfloat16)

    ax_copies = [send(az.at[0], ax.at[0], ctx=at(z, 1 - x))]
    az_copies = [send(az.at[0], az.at[k], ctx=at(zat(k), x)) for k in range(1, Z)]

    def project(piece, xx, k):
        first = pl.multiple_of(xx * half + zat(Z - k) * chunk, chunk)
        return jnp.dot(piece, wo[pl.ds(first, chunk), :], preferred_element_type=f32)

    locals_[3].wait()
    acc[...] = project(az[0], x, 0)
    for k in range(1, Z):
        az_copies[k - 1].wait_recv()
        ax_copies.append(send(az.at[k], ax.at[k], ctx=at(z, 1 - x)))
        acc[...] += project(az[k], x, k)
    for k in range(Z):
        ax_copies[k].wait_recv()
        acc[...] += project(ax[k], 1 - x, k)
    out_copies = []
    for d in range(1, nh):
        dest = lax.rem(h + d, nh)
        piece = acc.at[pl.ds(pl.multiple_of(dest * out_rows, out_rows), out_rows), :]
        out_copies.append(send(piece, orecv.at[d - 1], head=dest))
    mine = acc[pl.ds(pl.multiple_of(h * out_rows, out_rows), out_rows), :]
    for d in range(nh - 1):
        out_copies[d].wait_recv()
        mine = mine + orecv[d]
    out[...] = mine
    for cp in pending:
        cp.wait_send()


def fused(hidden, norm_gain, w_query, keys, values, w_output, valid_len, home_block):
    rows, feat = hidden.shape
    width = w_query.shape[1]
    cols = w_output.shape[1]
    nz, nh = lax.axis_size("ctx"), lax.axis_size("head")
    span = keys.shape[1]
    chunk = width // nz
    bf16, f32 = jnp.bfloat16, jnp.float32
    n_copies = (nz - 1) + 6 + 4 + 3 + 1 + 2 + 1 + 3 + 3 + (nh - 1)
    vmem = pl.BlockSpec(memory_space=pltpu.VMEM)
    hbm = pl.BlockSpec(memory_space=pl.ANY)
    return pl.pallas_call(
        fused_kernel,
        out_shape=jax.ShapeDtypeStruct((rows // nh, cols), f32),
        in_specs=[vmem, vmem, hbm, hbm, hbm, hbm, vmem, vmem],
        out_specs=vmem,
        scratch_shapes=[
            pltpu.VMEM(w_query.shape, bf16),
            pltpu.VMEM(w_output.shape, bf16),
            pltpu.VMEM((4, span, HD), bf16),
            pltpu.VMEM((4, span, HD), bf16),
            pltpu.VMEM((4, HD, span), bf16),
            pltpu.VMEM((rows, feat), bf16),
            pltpu.VMEM((nz, 8, 128), f32),
            pltpu.VMEM((Z, rows, chunk), f32),
            pltpu.VMEM((Z, rows, chunk), f32),
            pltpu.VMEM((Z, rows, chunk), f32),
            pltpu.VMEM((Z - 1, rows, chunk), f32),
            pltpu.VMEM((Z - 1, rows, chunk), f32),
            pltpu.VMEM((2, rows, chunk), bf16),
            pltpu.VMEM((4, span, rows), f32),
            pltpu.VMEM((2, chunk // HD, HD, rows), f32),
            pltpu.VMEM((2, 8, rows), f32),
            pltpu.VMEM((chunk // HD, HD, rows), f32),
            pltpu.VMEM((8, rows), f32),
            pltpu.VMEM((Z, rows, chunk), bf16),
            pltpu.VMEM((Z, rows, chunk), bf16),
            pltpu.VMEM((rows, cols), f32),
            pltpu.VMEM((nh - 1, rows // nh, cols), f32),
            pltpu.SemaphoreType.DMA((4,)),
            pltpu.SemaphoreType.DMA((n_copies,)),
            pltpu.SemaphoreType.DMA((n_copies,)),
        ],
        compiler_params=pltpu.CompilerParams(
            collective_id=0, has_side_effects=True, vmem_limit_bytes=48 * 1024 * 1024
        ),
    )(
        hidden, norm_gain.reshape(1, -1), w_query, keys, values, w_output,
        valid_len.reshape(1, -1), home_block.reshape(1, -1),
    )


def shards(
    hidden, norm_gain, w_query, manifest_keys, manifest_values, w_output, valid_len, home_block
):
    ctx_count = lax.axis_size("ctx")
    ctx_index = lax.axis_index("ctx")
    head_index = lax.axis_index("head")
    rows, feat = hidden.shape
    d_model = feat * ctx_count
    width = w_query.shape[1]
    heads_here = width // HD
    group = H // KVH
    span = manifest_keys.shape[1]
    hsplit = min(ctx_count, heads_here)
    rsplit = ctx_count // hsplit
    rows_dev = rows // rsplit
    heads_dev = heads_here // hsplit

    widened = hidden.astype(jnp.float32)
    total_sq = lax.psum(jnp.sum(widened * widened, axis=1, keepdims=True), "ctx")
    inv_rms = lax.rsqrt(total_sq / d_model + 1e-05)
    gain = lax.dynamic_slice_in_dim(norm_gain, ctx_index * feat, feat, 0)
    normed = (widened * inv_rms * gain[None, :]).astype(jnp.bfloat16)
    partial = jnp.dot(normed, w_query, preferred_element_type=jnp.float32)
    partial = partial.reshape(rsplit, rows_dev, hsplit, heads_dev * HD).transpose(2, 0, 1, 3)
    partial = partial.reshape(ctx_count, rows_dev, heads_dev * HD)
    query = lax.psum_scatter(partial, "ctx", scatter_dimension=0, tiled=False).astype(jnp.bfloat16)

    dest_heads = head_index * heads_here + (jnp.arange(ctx_count) // rsplit) * heads_dev
    dest_kv = dest_heads // group
    kv = jnp.stack([manifest_keys[dest_kv], manifest_values[dest_kv]], axis=1)
    kv = lax.all_to_all(kv, "ctx", split_axis=0, concat_axis=0, tiled=True)
    kv = kv.transpose(1, 0, 2, 3).reshape(2, ctx_count * span, HD)
    keys, values = kv[0], kv[1]

    first_row = (ctx_index % rsplit) * rows_dev
    lens = lax.dynamic_slice_in_dim(valid_len, first_row, rows_dev, 0)
    blocks = lax.dynamic_slice_in_dim(home_block, first_row, rows_dev, 0)
    places = jnp.arange(ctx_count * span, dtype=jnp.int32)
    usable = (places[None, :] < lens[:, None]) | ((places // span)[None, :] == blocks[:, None])
    usable = usable[:, None, :]
    q3 = query.reshape(rows_dev, heads_dev, HD)
    scores = jnp.einsum("nhd,jd->nhj", q3, keys, preferred_element_type=jnp.float32) * (
        1.0 / math.sqrt(HD)
    )
    scores = jnp.where(usable, scores, -1e30)
    row_max = jnp.max(scores, axis=2, keepdims=True)
    expo = jnp.where(usable, jnp.exp(scores - row_max), 0.0)
    row_sum = jnp.sum(expo, axis=2, keepdims=True)
    weighted = jnp.einsum(
        "nhj,jd->nhd", expo.astype(jnp.bfloat16), values, preferred_element_type=jnp.float32
    )
    attn = (weighted / row_sum).astype(jnp.bfloat16).reshape(rows_dev, heads_dev * HD)
    attn = lax.all_gather(attn, "ctx", axis=0, tiled=False)
    attn = attn.reshape(hsplit, rsplit, rows_dev, heads_dev * HD).transpose(1, 2, 0, 3)
    attn = attn.reshape(rows, width)
    return lax.psum_scatter(
        jnp.dot(attn, w_output, preferred_element_type=jnp.float32),
        "head",
        scatter_dimension=0,
        tiled=True,
    )


def solution(mesh):
    in_specs = (
        P(None, "ctx"),
        P(),
        P("ctx", "head"),
        P(None, "ctx", None),
        P(None, "ctx", None),
        P("head", "ctx"),
        P(),
        P(),
    )
    out_specs = P("head", "ctx")
    small = mesh.shape["ctx"] == Z * X and mesh.shape["head"] * X == KVH
    return jax.shard_map(fused if small else shards, mesh=mesh, in_specs=in_specs, out_specs=out_specs, check_vma=False)
```

```python
import math

import jax
import jax.numpy as jnp
from jax import lax
from jax.experimental import pallas as pl
from jax.experimental.pallas import tpu as pltpu
from jax.sharding import PartitionSpec as P

H = 64
KVH = 8
HD = 128

Z = 4
X = 2


def fused_kernel(
    hidden, gain, wq_hbm, k_hbm, v_hbm, wo_hbm, lens, home, out,
    wq, wo, kb, vb, vt, nrm, sq, xsend, xrecv, qown, zsend, zrecv, qb, sc,
    os_, st, ocr, scr, az, ax, acc, orecv, ysend, local_sem, send_sem, recv_sem,
):
    c = lax.axis_index("ctx")
    h = lax.axis_index("head")
    z, x = lax.div(c, X), lax.rem(c, X)
    nz = lax.axis_size("ctx")
    nh = lax.axis_size("head")
    rows, feat = hidden.shape
    span = kb.shape[1]
    chunk = qb.shape[2]
    out_rows = out.shape[0]
    per_chunk = chunk // HD
    scale = 1.0 / math.sqrt(HD)
    f32 = jnp.float32
    pending = []
    next_sem = [0]

    def at(zz, xx):
        return zz * X + xx

    def send(src, dst, **where):
        i = next_sem[0]
        next_sem[0] += 1
        copy = pltpu.make_async_remote_copy(
            src_ref=src, dst_ref=dst, send_sem=send_sem.at[i], recv_sem=recv_sem.at[i],
            device_id=where, device_id_type=pl.DeviceIdType.MESH,
        )
        copy.start()
        pending.append(copy)
        return copy

    def zat(k):
        return lax.rem(z + k, Z)

    barrier = pltpu.get_barrier_semaphore()
    for k in range(1, nz):
        pl.semaphore_signal(barrier, inc=1, device_id={"ctx": lax.rem(c + k, nz)}, device_id_type=pl.DeviceIdType.MESH)
    for k in range(1, nh):
        pl.semaphore_signal(barrier, inc=1, device_id={"head": lax.rem(h + k, nh)}, device_id_type=pl.DeviceIdType.MESH)

    kv_mine = h * X + lax.div(z, X)
    locals_ = [
        pltpu.make_async_copy(wq_hbm, wq, local_sem.at[0]),
        pltpu.make_async_copy(k_hbm.at[kv_mine], kb.at[0], local_sem.at[1]),
        pltpu.make_async_copy(v_hbm.at[kv_mine], vb.at[0], local_sem.at[2]),
        pltpu.make_async_copy(wo_hbm, wo, local_sem.at[3]),
    ]
    for cp in locals_:
        cp.start()

    eye = lax.broadcasted_iota(jnp.int32, (128, 128), 0) == lax.broadcasted_iota(jnp.int32, (128, 128), 1)
    wide = hidden[...].astype(f32)
    col = jnp.sum(wide * wide, axis=1, keepdims=True)
    pieces = [
        jnp.sum(jnp.where(eye, col[b * 128 : (b + 1) * 128], 0.0), axis=0, keepdims=True)
        for b in range(rows // 128)
    ]
    pieces.append(jnp.zeros((8 - rows // 128, 128), f32))
    sq[0] = jnp.concatenate(pieces, axis=0)
    pl.semaphore_wait(barrier, nz - 1 + nh - 1)
    sq_copies = [send(sq.at[0], sq.at[k], ctx=lax.rem(c + k, nz)) for k in range(1, nz)]
    kv_copies = []
    for k in range(1, Z):
        idx = h * X + lax.div(zat(k), X)
        kv_copies.append(send(k_hbm.at[idx], kb.at[k], ctx=at(zat(k), x)))
        kv_copies.append(send(v_hbm.at[idx], vb.at[k], ctx=at(zat(k), x)))
    for cp in sq_copies:
        cp.wait_recv()
    total = sq[0]
    for k in range(1, nz):
        total = total + sq[k]
    inv = lax.rsqrt(total / (feat * nz) + 1e-05)
    for b in range(rows // 128):
        inv_col = jnp.sum(jnp.where(eye, inv[b : b + 1, :], 0.0), axis=1, keepdims=True)
        blk = hidden[b * 128 : (b + 1) * 128, :].astype(f32)
        g = gain[:, pl.ds(pl.multiple_of(c * feat, feat), feat)]
        nrm[b * 128 : (b + 1) * 128, :] = (blk * inv_col * g).astype(jnp.bfloat16)

    def part(xx, k):
        cols = pl.ds(pl.multiple_of(at(zat(k), xx) * chunk, chunk), chunk)
        return jnp.dot(nrm[...], wq[:, cols], preferred_element_type=f32)

    locals_[0].wait()
    x_copies = {}
    for k in (1, 2, 3, 0):
        xsend[k] = part(1 - x, k)
        x_copies[k] = send(xsend.at[k], xrecv.at[k], ctx=at(z, 1 - x))
    for k in (1, 2, 3, 0):
        qown[k] = part(x, k)
    z_copies = []
    for k in (1, 2, 3):
        x_copies[k].wait_recv()
        zsend[k - 1] = qown[k] + xrecv[k]
        z_copies.append(send(zsend.at[k - 1], zrecv.at[k - 1], ctx=at(zat(k), x)))

    locals_[1].wait()
    locals_[2].wait()
    for cp in kv_copies:
        cp.wait_recv()
    for s in range(Z):
        vt[s] = vb[s].astype(f32).T.astype(jnp.bfloat16)

    x_copies[0].wait_recv()
    qsum = qown[0] + xrecv[0]
    for k in range(3):
        z_copies[k].wait_recv()
        qsum = qsum + zrecv[k]
    qb[0] = qsum.astype(jnp.bfloat16)
    beside = at(z, 1 - x)
    q_copy = send(qb.at[0], qb.at[1], ctx=beside)

    place = lax.broadcasted_iota(jnp.int32, (span, rows), 0)
    owners = [at(zat(Z - k), x) for k in range(Z)]

    def attend(i):
        copies = []
        for j in range(per_chunk):
            q_head = qb[i, :, j * HD : (j + 1) * HD]
            top = jnp.full((1, rows), -1e30, f32)
            for s in range(Z):
                limit = jnp.where(home[...] == owners[s], span, lens[...] - owners[s] * span)
                raw = lax.dot_general(kb[s], q_head, (((1,), (1,)), ((), ())), preferred_element_type=f32)
                raw = jnp.where(place < limit, raw, -1e30)
                sc[s] = raw
                top = jnp.maximum(top, jnp.max(raw, axis=0, keepdims=True))
            tot = jnp.zeros((1, rows), f32)
            acc_o = jnp.zeros((HD, rows), f32)
            for s in range(Z):
                e = jnp.exp((sc[s] - top) * scale)
                tot = tot + jnp.sum(e, axis=0, keepdims=True)
                acc_o = acc_o + jnp.dot(vt[s], e.astype(jnp.bfloat16), preferred_element_type=f32)
            os_[i, j] = acc_o
            st[i, j, 0:1, :] = top
            st[i, j, 1:2, :] = tot
            if i == 1:
                copies.append(send(os_.at[1, j], ocr.at[j], ctx=beside))
                copies.append(send(st.at[1, j], scr.at[j], ctx=beside))
        return copies

    st[...] = jnp.zeros_like(st)
    attend(0)
    q_copy.wait_recv()
    state_copies = attend(1)
    ax_copies, az_copies = {}, {}
    for j in range(per_chunk):
        state_copies[2 * j].wait_recv()
        state_copies[2 * j + 1].wait_recv()
        m0, m1 = st[0, j, 0:1, :], scr[j, 0:1, :]
        l0, l1 = st[0, j, 1:2, :], scr[j, 1:2, :]
        m = jnp.maximum(m0, m1)
        a0, a1 = jnp.exp((m0 - m) * scale), jnp.exp((m1 - m) * scale)
        res = (a0 * os_[0, j] + a1 * ocr[j]) / (a0 * l0 + a1 * l1)
        az[j, 0] = res.T.astype(jnp.bfloat16)
        for k in range(1, Z):
            az_copies[j, k] = send(az.at[j, 0], az.at[j, k], ctx=at(zat(k), x))
        ax_copies[j, 0] = send(az.at[j, 0], ax.at[j, 0], ctx=beside)

    def project(piece, xx, j, k):
        first = pl.multiple_of(at(zat(Z - k), xx) * chunk + j * HD, HD)
        return jnp.dot(piece, wo[pl.ds(first, HD), :], preferred_element_type=f32)

    locals_[3].wait()
    for j in range(per_chunk):
        if j == 0:
            acc[...] = project(az[j, 0], x, j, 0)
        else:
            acc[...] += project(az[j, 0], x, j, 0)
    for j in range(per_chunk):
        for k in range(1, Z):
            az_copies[j, k].wait_recv()
            ax_copies[j, k] = send(az.at[j, k], ax.at[j, k], ctx=beside)
            acc[...] += project(az[j, k], x, j, k)
    for j in range(per_chunk):
        for k in range(Z):
            ax_copies[j, k].wait_recv()
            acc[...] += project(ax[j, k], 1 - x, j, k)

    y, core = lax.div(h, 2), lax.rem(h, 2)

    def rows_of(head):
        return pl.ds(pl.multiple_of(head * out_rows, out_rows), out_rows)

    other_core = y * 2 + 1 - core
    other_y = (1 - y) * 2 + core
    first_core = send(acc.at[rows_of((1 - y) * 2 + 1 - core), :], orecv.at[0], head=other_core)
    second_core = send(acc.at[rows_of(other_core), :], orecv.at[1], head=other_core)
    first_core.wait_recv()
    ysend[...] = acc[rows_of(other_y), :] + orecv[0]
    y_copy = send(ysend, orecv.at[2], head=other_y)
    second_core.wait_recv()
    mine = acc[rows_of(h), :] + orecv[1]
    y_copy.wait_recv()
    out[...] = mine + orecv[2]
    for cp in pending:
        cp.wait_send()


def fused(hidden, norm_gain, w_query, keys, values, w_output, valid_len, home_block):
    rows, feat = hidden.shape
    width = w_query.shape[1]
    cols = w_output.shape[1]
    nz, nh = lax.axis_size("ctx"), lax.axis_size("head")
    span = keys.shape[1]
    chunk = width // nz
    bf16, f32 = jnp.bfloat16, jnp.float32
    per = chunk // HD
    n_copies = (nz - 1) + 6 + 4 + 3 + 1 + 2 * per + 7 * per + 3
    vmem = pl.BlockSpec(memory_space=pltpu.VMEM)
    hbm = pl.BlockSpec(memory_space=pltpu.HBM)
    return pl.pallas_call(
        fused_kernel,
        out_shape=jax.ShapeDtypeStruct((rows // nh, cols), f32),
        in_specs=[vmem, vmem, hbm, hbm, hbm, hbm, vmem, vmem],
        out_specs=vmem,
        scratch_shapes=[
            pltpu.VMEM(w_query.shape, bf16),
            pltpu.VMEM(w_output.shape, bf16),
            pltpu.VMEM((4, span, HD), bf16),
            pltpu.VMEM((4, span, HD), bf16),
            pltpu.VMEM((4, HD, span), bf16),
            pltpu.VMEM((rows, feat), bf16),
            pltpu.VMEM((nz, 8, 128), f32),
            pltpu.VMEM((Z, rows, chunk), f32),
            pltpu.VMEM((Z, rows, chunk), f32),
            pltpu.VMEM((Z, rows, chunk), f32),
            pltpu.VMEM((Z - 1, rows, chunk), f32),
            pltpu.VMEM((Z - 1, rows, chunk), f32),
            pltpu.VMEM((2, rows, chunk), bf16),
            pltpu.VMEM((4, span, rows), f32),
            pltpu.VMEM((2, per, HD, rows), f32),
            pltpu.VMEM((2, per, 8, rows), f32),
            pltpu.VMEM((per, HD, rows), f32),
            pltpu.VMEM((per, 8, rows), f32),
            pltpu.VMEM((per, Z, rows, HD), bf16),
            pltpu.VMEM((per, Z, rows, HD), bf16),
            pltpu.VMEM((rows, cols), f32),
            pltpu.VMEM((3, rows // nh, cols), f32),
            pltpu.VMEM((rows // nh, cols), f32),
            pltpu.SemaphoreType.DMA((4,)),
            pltpu.SemaphoreType.DMA((n_copies,)),
            pltpu.SemaphoreType.DMA((n_copies,)),
        ],
        compiler_params=pltpu.CompilerParams(
            collective_id=0, has_side_effects=True, vmem_limit_bytes=48 * 1024 * 1024
        ),
    )(
        hidden, norm_gain.reshape(1, -1), w_query, keys, values, w_output,
        valid_len.reshape(1, -1), home_block.reshape(1, -1),
    )


def shards(
    hidden, norm_gain, w_query, manifest_keys, manifest_values, w_output, valid_len, home_block
):
    ctx_count = lax.axis_size("ctx")
    ctx_index = lax.axis_index("ctx")
    head_index = lax.axis_index("head")
    rows, feat = hidden.shape
    d_model = feat * ctx_count
    width = w_query.shape[1]
    heads_here = width // HD
    group = H // KVH
    span = manifest_keys.shape[1]
    hsplit = min(ctx_count, heads_here)
    rsplit = ctx_count // hsplit
    rows_dev = rows // rsplit
    heads_dev = heads_here // hsplit

    widened = hidden.astype(jnp.float32)
    total_sq = lax.psum(jnp.sum(widened * widened, axis=1, keepdims=True), "ctx")
    inv_rms = lax.rsqrt(total_sq / d_model + 1e-05)
    gain = lax.dynamic_slice_in_dim(norm_gain, ctx_index * feat, feat, 0)
    normed = (widened * inv_rms * gain[None, :]).astype(jnp.bfloat16)
    partial = jnp.dot(normed, w_query, preferred_element_type=jnp.float32)
    partial = partial.reshape(rsplit, rows_dev, hsplit, heads_dev * HD).transpose(2, 0, 1, 3)
    partial = partial.reshape(ctx_count, rows_dev, heads_dev * HD)
    query = lax.psum_scatter(partial, "ctx", scatter_dimension=0, tiled=False).astype(jnp.bfloat16)

    dest_heads = head_index * heads_here + (jnp.arange(ctx_count) // rsplit) * heads_dev
    dest_kv = dest_heads // group
    kv = jnp.stack([manifest_keys[dest_kv], manifest_values[dest_kv]], axis=1)
    kv = lax.all_to_all(kv, "ctx", split_axis=0, concat_axis=0, tiled=True)
    kv = kv.transpose(1, 0, 2, 3).reshape(2, ctx_count * span, HD)
    keys, values = kv[0], kv[1]

    first_row = (ctx_index % rsplit) * rows_dev
    lens = lax.dynamic_slice_in_dim(valid_len, first_row, rows_dev, 0)
    blocks = lax.dynamic_slice_in_dim(home_block, first_row, rows_dev, 0)
    places = jnp.arange(ctx_count * span, dtype=jnp.int32)
    usable = (places[None, :] < lens[:, None]) | ((places // span)[None, :] == blocks[:, None])
    usable = usable[:, None, :]
    q3 = query.reshape(rows_dev, heads_dev, HD)
    scores = jnp.einsum("nhd,jd->nhj", q3, keys, preferred_element_type=jnp.float32) * (
        1.0 / math.sqrt(HD)
    )
    scores = jnp.where(usable, scores, -1e30)
    row_max = jnp.max(scores, axis=2, keepdims=True)
    expo = jnp.where(usable, jnp.exp(scores - row_max), 0.0)
    row_sum = jnp.sum(expo, axis=2, keepdims=True)
    weighted = jnp.einsum(
        "nhj,jd->nhd", expo.astype(jnp.bfloat16), values, preferred_element_type=jnp.float32
    )
    attn = (weighted / row_sum).astype(jnp.bfloat16).reshape(rows_dev, heads_dev * HD)
    attn = lax.all_gather(attn, "ctx", axis=0, tiled=False)
    attn = attn.reshape(hsplit, rsplit, rows_dev, heads_dev * HD).transpose(1, 2, 0, 3)
    attn = attn.reshape(rows, width)
    return lax.psum_scatter(
        jnp.dot(attn, w_output, preferred_element_type=jnp.float32),
        "head",
        scatter_dimension=0,
        tiled=True,
    )


def solution(mesh):
    in_specs = (
        P(None, "ctx"),
        P(),
        P("ctx", "head"),
        P(None, "ctx", None),
        P(None, "ctx", None),
        P("head", "ctx"),
        P(),
        P(),
    )
    out_specs = P("head", "ctx")
    small = mesh.shape["ctx"] == Z * X and mesh.shape["head"] * X == KVH
    return jax.shard_map(fused if small else shards, mesh=mesh, in_specs=in_specs, out_specs=out_specs, check_vma=False)
```

```python
import math

import jax
import jax.numpy as jnp
from jax import lax
from jax.experimental import pallas as pl
from jax.experimental.pallas import tpu as pltpu
from jax.sharding import PartitionSpec as P

H = 64
KVH = 8
HD = 128

Z = 4
X = 2


def fused_kernel(
    hidden, gain, wq_hbm, k_hbm, v_hbm, wo_hbm, lens, home, out,
    wq, wo, kb, vb, vt, nrm, sq, xsend, xrecv, qown, zsend, zrecv, qb, sc,
    os_, st, ocr, scr, az, ax, acc, orecv, ysend, local_sem, send_sem, recv_sem,
):
    c = lax.axis_index("ctx")
    h = lax.axis_index("head")
    z, x = lax.div(c, X), lax.rem(c, X)
    nz = lax.axis_size("ctx")
    nh = lax.axis_size("head")
    rows, feat = hidden.shape
    span = kb.shape[1]
    chunk = qb.shape[2]
    half = chunk * Z
    out_rows = out.shape[0]
    per_chunk = chunk // HD
    scale = 1.0 / math.sqrt(HD)
    f32 = jnp.float32
    pending = []
    next_sem = [0]

    def at(zz, xx):
        return zz * X + xx

    def send(src, dst, **where):
        i = next_sem[0]
        next_sem[0] += 1
        copy = pltpu.make_async_remote_copy(
            src_ref=src, dst_ref=dst, send_sem=send_sem.at[i], recv_sem=recv_sem.at[i],
            device_id=where, device_id_type=pl.DeviceIdType.MESH,
        )
        copy.start()
        pending.append(copy)
        return copy

    def zat(k):
        return lax.rem(z + k, Z)

    barrier = pltpu.get_barrier_semaphore()
    for k in range(1, nz):
        pl.semaphore_signal(barrier, inc=1, device_id={"ctx": lax.rem(c + k, nz)}, device_id_type=pl.DeviceIdType.MESH)
    for k in range(1, nh):
        pl.semaphore_signal(barrier, inc=1, device_id={"head": lax.rem(h + k, nh)}, device_id_type=pl.DeviceIdType.MESH)

    kv_mine = h * X + x
    kv_other = h * X + (1 - x)
    locals_ = [
        pltpu.make_async_copy(wq_hbm, wq, local_sem.at[0]),
        pltpu.make_async_copy(k_hbm.at[kv_mine], kb.at[0], local_sem.at[1]),
        pltpu.make_async_copy(v_hbm.at[kv_mine], vb.at[0], local_sem.at[2]),
        pltpu.make_async_copy(wo_hbm, wo, local_sem.at[3]),
    ]
    for cp in locals_:
        cp.start()

    eye = lax.broadcasted_iota(jnp.int32, (128, 128), 0) == lax.broadcasted_iota(jnp.int32, (128, 128), 1)
    wide = hidden[...].astype(f32)
    col = jnp.sum(wide * wide, axis=1, keepdims=True)
    pieces = [
        jnp.sum(jnp.where(eye, col[b * 128 : (b + 1) * 128], 0.0), axis=0, keepdims=True)
        for b in range(rows // 128)
    ]
    pieces.append(jnp.zeros((8 - rows // 128, 128), f32))
    sq[0] = jnp.concatenate(pieces, axis=0)
    pl.semaphore_wait(barrier, nz - 1 + nh - 1)
    sq_copies = [send(sq.at[0], sq.at[k], ctx=lax.rem(c + k, nz)) for k in range(1, nz)]
    zp = z + 1 - 2 * lax.rem(z, 2)

    def send_kv(idx, slot, zz, xx):
        return [
            send(k_hbm.at[idx], kb.at[slot], ctx=at(zz, xx)),
            send(v_hbm.at[idx], vb.at[slot], ctx=at(zz, xx)),
        ]

    kv_near = send_kv(kv_mine, 2, zp, x)
    for cp in sq_copies:
        cp.wait_recv()
    total = sq[0]
    for k in range(1, nz):
        total = total + sq[k]
    inv = lax.rsqrt(total / (feat * nz) + 1e-05)
    for b in range(rows // 128):
        inv_col = jnp.sum(jnp.where(eye, inv[b : b + 1, :], 0.0), axis=1, keepdims=True)
        blk = hidden[b * 128 : (b + 1) * 128, :].astype(f32)
        g = gain[:, pl.ds(pl.multiple_of(c * feat, feat), feat)]
        nrm[b * 128 : (b + 1) * 128, :] = (blk * inv_col * g).astype(jnp.bfloat16)

    def part(xx, k):
        cols = pl.ds(pl.multiple_of(xx * half + zat(k) * chunk, chunk), chunk)
        return jnp.dot(nrm[...], wq[:, cols], preferred_element_type=f32)

    locals_[0].wait()
    x_copies = {}
    for k in (1, 2, 3, 0):
        xsend[k] = part(1 - x, k)
        x_copies[k] = send(xsend.at[k], xrecv.at[k], ctx=at(z, 1 - x))
    kv_far = send_kv(kv_other, 1, z, 1 - x) + send_kv(kv_other, 3, zp, 1 - x)
    for k in (1, 2, 3, 0):
        qown[k] = part(x, k)
    z_copies = []
    for k in (1, 2, 3):
        x_copies[k].wait_recv()
        zsend[k - 1] = qown[k] + xrecv[k]
        z_copies.append(send(zsend.at[k - 1], zrecv.at[k - 1], ctx=at(zat(k), x)))

    locals_[1].wait()
    locals_[2].wait()
    for cp in kv_near:
        cp.wait_recv()
    for s in (0, 2):
        vt[s] = vb[s].astype(f32).T.astype(jnp.bfloat16)

    x_copies[0].wait_recv()
    qsum = qown[0] + xrecv[0]
    for k in range(3):
        z_copies[k].wait_recv()
        qsum = qsum + zrecv[k]
    qb[0] = qsum.astype(jnp.bfloat16)
    beside = at(z, 1 - x)
    far = at(zat(2), x)
    q_copy = send(qb.at[0], qb.at[1], ctx=far)
    for cp in kv_far:
        cp.wait_recv()
    for s in (1, 3):
        vt[s] = vb[s].astype(f32).T.astype(jnp.bfloat16)

    place = lax.broadcasted_iota(jnp.int32, (span, rows), 0)
    owners = (at(z, x), at(z, 1 - x), at(zp, x), at(zp, 1 - x))

    def attend(i):
        copies = []
        for j in range(per_chunk):
            q_head = qb[i, :, j * HD : (j + 1) * HD]
            top = jnp.full((1, rows), -1e30, f32)
            for s in range(Z):
                limit = jnp.where(home[...] == owners[s], span, lens[...] - owners[s] * span)
                raw = lax.dot_general(kb[s], q_head, (((1,), (1,)), ((), ())), preferred_element_type=f32)
                raw = jnp.where(place < limit, raw, -1e30)
                sc[s] = raw
                top = jnp.maximum(top, jnp.max(raw, axis=0, keepdims=True))
            tot = jnp.zeros((1, rows), f32)
            acc_o = jnp.zeros((HD, rows), f32)
            for s in range(Z):
                e = jnp.exp((sc[s] - top) * scale)
                tot = tot + jnp.sum(e, axis=0, keepdims=True)
                acc_o = acc_o + jnp.dot(vt[s], e.astype(jnp.bfloat16), preferred_element_type=f32)
            os_[i, j] = acc_o
            st[i, j, 0:1, :] = top
            st[i, j, 1:2, :] = tot
            if i == 1:
                copies.append(send(os_.at[1, j], ocr.at[j], ctx=far))
                copies.append(send(st.at[1, j], scr.at[j], ctx=far))
        return copies

    st[...] = jnp.zeros_like(st)
    attend(0)
    q_copy.wait_recv()
    state_copies = attend(1)
    ax_copies, az_copies = {}, {}
    for j in range(per_chunk):
        state_copies[2 * j].wait_recv()
        state_copies[2 * j + 1].wait_recv()
        m0, m1 = st[0, j, 0:1, :], scr[j, 0:1, :]
        l0, l1 = st[0, j, 1:2, :], scr[j, 1:2, :]
        m = jnp.maximum(m0, m1)
        a0, a1 = jnp.exp((m0 - m) * scale), jnp.exp((m1 - m) * scale)
        res = (a0 * os_[0, j] + a1 * ocr[j]) / (a0 * l0 + a1 * l1)
        az[j, 0] = res.T.astype(jnp.bfloat16)
        for k in range(1, Z):
            az_copies[j, k] = send(az.at[j, 0], az.at[j, k], ctx=at(zat(k), x))
        ax_copies[j, 0] = send(az.at[j, 0], ax.at[j, 0], ctx=beside)

    def project(piece, xx, j, k):
        first = pl.multiple_of(xx * half + zat(Z - k) * chunk + j * HD, HD)
        return jnp.dot(piece, wo[pl.ds(first, HD), :], preferred_element_type=f32)

    locals_[3].wait()
    for j in range(per_chunk):
        if j == 0:
            acc[...] = project(az[j, 0], x, j, 0)
        else:
            acc[...] += project(az[j, 0], x, j, 0)
    for j in range(per_chunk):
        for k in range(1, Z):
            az_copies[j, k].wait_recv()
            ax_copies[j, k] = send(az.at[j, k], ax.at[j, k], ctx=beside)
            acc[...] += project(az[j, k], x, j, k)
    for j in range(per_chunk):
        for k in range(Z):
            ax_copies[j, k].wait_recv()
            acc[...] += project(ax[j, k], 1 - x, j, k)

    y, core = lax.div(h, 2), lax.rem(h, 2)

    def rows_of(head):
        return pl.ds(pl.multiple_of(head * out_rows, out_rows), out_rows)

    other_core = y * 2 + 1 - core
    other_y = (1 - y) * 2 + core
    first_core = send(acc.at[rows_of((1 - y) * 2 + 1 - core), :], orecv.at[0], head=other_core)
    second_core = send(acc.at[rows_of(other_core), :], orecv.at[1], head=other_core)
    first_core.wait_recv()
    ysend[...] = acc[rows_of(other_y), :] + orecv[0]
    y_copy = send(ysend, orecv.at[2], head=other_y)
    second_core.wait_recv()
    mine = acc[rows_of(h), :] + orecv[1]
    y_copy.wait_recv()
    out[...] = mine + orecv[2]
    for cp in pending:
        cp.wait_send()


def fused(hidden, norm_gain, w_query, keys, values, w_output, valid_len, home_block):
    rows, feat = hidden.shape
    width = w_query.shape[1]
    cols = w_output.shape[1]
    nz, nh = lax.axis_size("ctx"), lax.axis_size("head")
    span = keys.shape[1]
    chunk = width // nz
    bf16, f32 = jnp.bfloat16, jnp.float32
    per = chunk // HD
    n_copies = (nz - 1) + 6 + 4 + 3 + 1 + 2 * per + 7 * per + 3
    vmem = pl.BlockSpec(memory_space=pltpu.VMEM)
    hbm = pl.BlockSpec(memory_space=pltpu.HBM)
    return pl.pallas_call(
        fused_kernel,
        out_shape=jax.ShapeDtypeStruct((rows // nh, cols), f32),
        in_specs=[vmem, vmem, hbm, hbm, hbm, hbm, vmem, vmem],
        out_specs=vmem,
        scratch_shapes=[
            pltpu.VMEM(w_query.shape, bf16),
            pltpu.VMEM(w_output.shape, bf16),
            pltpu.VMEM((4, span, HD), bf16),
            pltpu.VMEM((4, span, HD), bf16),
            pltpu.VMEM((4, HD, span), bf16),
            pltpu.VMEM((rows, feat), bf16),
            pltpu.VMEM((nz, 8, 128), f32),
            pltpu.VMEM((Z, rows, chunk), f32),
            pltpu.VMEM((Z, rows, chunk), f32),
            pltpu.VMEM((Z, rows, chunk), f32),
            pltpu.VMEM((Z - 1, rows, chunk), f32),
            pltpu.VMEM((Z - 1, rows, chunk), f32),
            pltpu.VMEM((2, rows, chunk), bf16),
            pltpu.VMEM((4, span, rows), f32),
            pltpu.VMEM((2, per, HD, rows), f32),
            pltpu.VMEM((2, per, 8, rows), f32),
            pltpu.VMEM((per, HD, rows), f32),
            pltpu.VMEM((per, 8, rows), f32),
            pltpu.VMEM((per, Z, rows, HD), bf16),
            pltpu.VMEM((per, Z, rows, HD), bf16),
            pltpu.VMEM((rows, cols), f32),
            pltpu.VMEM((3, rows // nh, cols), f32),
            pltpu.VMEM((rows // nh, cols), f32),
            pltpu.SemaphoreType.DMA((4,)),
            pltpu.SemaphoreType.DMA((n_copies,)),
            pltpu.SemaphoreType.DMA((n_copies,)),
        ],
        compiler_params=pltpu.CompilerParams(
            collective_id=0, has_side_effects=True, vmem_limit_bytes=48 * 1024 * 1024
        ),
    )(
        hidden, norm_gain.reshape(1, -1), w_query, keys, values, w_output,
        valid_len.reshape(1, -1), home_block.reshape(1, -1),
    )


def shards(
    hidden, norm_gain, w_query, manifest_keys, manifest_values, w_output, valid_len, home_block
):
    ctx_count = lax.axis_size("ctx")
    ctx_index = lax.axis_index("ctx")
    head_index = lax.axis_index("head")
    rows, feat = hidden.shape
    d_model = feat * ctx_count
    width = w_query.shape[1]
    heads_here = width // HD
    group = H // KVH
    span = manifest_keys.shape[1]
    hsplit = min(ctx_count, heads_here)
    rsplit = ctx_count // hsplit
    rows_dev = rows // rsplit
    heads_dev = heads_here // hsplit

    widened = hidden.astype(jnp.float32)
    total_sq = lax.psum(jnp.sum(widened * widened, axis=1, keepdims=True), "ctx")
    inv_rms = lax.rsqrt(total_sq / d_model + 1e-05)
    gain = lax.dynamic_slice_in_dim(norm_gain, ctx_index * feat, feat, 0)
    normed = (widened * inv_rms * gain[None, :]).astype(jnp.bfloat16)
    partial = jnp.dot(normed, w_query, preferred_element_type=jnp.float32)
    partial = partial.reshape(rsplit, rows_dev, hsplit, heads_dev * HD).transpose(2, 0, 1, 3)
    partial = partial.reshape(ctx_count, rows_dev, heads_dev * HD)
    query = lax.psum_scatter(partial, "ctx", scatter_dimension=0, tiled=False).astype(jnp.bfloat16)

    dest_heads = head_index * heads_here + (jnp.arange(ctx_count) // rsplit) * heads_dev
    dest_kv = dest_heads // group
    kv = jnp.stack([manifest_keys[dest_kv], manifest_values[dest_kv]], axis=1)
    kv = lax.all_to_all(kv, "ctx", split_axis=0, concat_axis=0, tiled=True)
    kv = kv.transpose(1, 0, 2, 3).reshape(2, ctx_count * span, HD)
    keys, values = kv[0], kv[1]

    first_row = (ctx_index % rsplit) * rows_dev
    lens = lax.dynamic_slice_in_dim(valid_len, first_row, rows_dev, 0)
    blocks = lax.dynamic_slice_in_dim(home_block, first_row, rows_dev, 0)
    places = jnp.arange(ctx_count * span, dtype=jnp.int32)
    usable = (places[None, :] < lens[:, None]) | ((places // span)[None, :] == blocks[:, None])
    usable = usable[:, None, :]
    q3 = query.reshape(rows_dev, heads_dev, HD)
    scores = jnp.einsum("nhd,jd->nhj", q3, keys, preferred_element_type=jnp.float32) * (
        1.0 / math.sqrt(HD)
    )
    scores = jnp.where(usable, scores, -1e30)
    row_max = jnp.max(scores, axis=2, keepdims=True)
    expo = jnp.where(usable, jnp.exp(scores - row_max), 0.0)
    row_sum = jnp.sum(expo, axis=2, keepdims=True)
    weighted = jnp.einsum(
        "nhj,jd->nhd", expo.astype(jnp.bfloat16), values, preferred_element_type=jnp.float32
    )
    attn = (weighted / row_sum).astype(jnp.bfloat16).reshape(rows_dev, heads_dev * HD)
    attn = lax.all_gather(attn, "ctx", axis=0, tiled=False)
    attn = attn.reshape(hsplit, rsplit, rows_dev, heads_dev * HD).transpose(1, 2, 0, 3)
    attn = attn.reshape(rows, width)
    return lax.psum_scatter(
        jnp.dot(attn, w_output, preferred_element_type=jnp.float32),
        "head",
        scatter_dimension=0,
        tiled=True,
    )


def solution(mesh):
    in_specs = (
        P(None, "ctx"),
        P(),
        P("ctx", "head"),
        P(None, "ctx", None),
        P(None, "ctx", None),
        P("head", "ctx"),
        P(),
        P(),
    )
    out_specs = P("head", "ctx")
    small = mesh.shape["ctx"] == Z * X and mesh.shape["head"] * X == KVH
    return jax.shard_map(fused if small else shards, mesh=mesh, in_specs=in_specs, out_specs=out_specs, check_vma=False)
```
